32 devices in a mesh: groups: 2 (over x), row: 8 (over z, y), col: 2 (over core).
Axes of the slice: x: 2, y: 2, z: 4, core: 2. Of those that a mesh axis runs over, the one named last changes fastest.
Arguments:
- prefix_states: bfloat16 [2048, 8192], P(('groups', 'col'), 'row'), parts along dimension 0, may hold values from -480 to 480
- prefix_gain: float32 [8192], P('row'), may hold values from 0.1 to 1.9
- backbone_key: bfloat16 [8192, 1024], P('row', 'col'), may hold values from -0.0625 to 0.0625
- backbone_value: bfloat16 [8192, 1024], P('row', 'col'), may hold values from -0.0625 to 0.0625
- action_states: bfloat16 [16384, 2048], P(('groups', 'row'), 'col'), parts along dimension 0, may hold values from -14 to 14
- expert_query: bfloat16 [2048, 2048], P('row', 'col'), may hold values from -0.25 to 0.25
- expert_key: bfloat16 [2048, 1024], P('row', 'col'), may hold values from -0.125 to 0.125
- expert_value: bfloat16 [2048, 1024], P('row', 'col'), may hold values from -0.125 to 0.125
- expert_out: bfloat16 [2048, 2048], P('col', 'row'), may hold values from -0.5 to 0.5
- prefix_length: int32 [16], P(('groups', 'row')), parts along dimension 0, may hold values from 32 to 128, as said below
- action_length: int32 [16], P(('groups', 'row')), parts along dimension 0, may hold values from 256 to 1024, as said below
Outputs:
- prefix_keys: bfloat16 [2048, 1024], P(('groups', 'row'), 'col'), parts along dimension 0
- prefix_values: bfloat16 [2048, 1024], P(('groups', 'row'), 'col'), parts along dimension 0
- action_out: bfloat16 [16384, 2048], P(('groups', 'row'), 'col'), parts along dimension 0
The draws below stay inside these ranges and needn't reach their ends.
There are 2 independent parts, one for each index of `groups`. The reference program is written for one: setup_inputs(seed, part) draws one part's arguments, and reference() takes and returns one part's arrays. A program takes and returns all parts, laid end to end along the dimension named above; an argument that names none is the same for every part. Nothing has to cross between parts.
Inputs may be any that keep to these rules, and one draw needn't show every extreme that they name: `prefix_length`: every draw has an episode with all 128 prefix tokens valid. `action_length`: every draw has an episode with all 1024 action tokens valid.
All inputs are finite; a program needn't handle non-finite values.
Results may differ from the reference program's by a relative error of at most 0.0095.
Values may be sent and summed in bfloat16 or wider, within the bound.
No kernel may reach another device: no remote copies, remote signals or barrier semaphores. Data moves between devices by JAX's collectives and lax.ppermute only.
A program may use at most 128 MiB of HBM per device.

```python
import math
import jax
import jax.numpy as jnp
from jax import lax

D = 8192
KV_HEADS = 8
HEAD = 128
DA = 2048
PREF = 128
ACT = 1024
KV = 1024
QW = 2048
EPISODES = 8


def draw_prefix_states(key, part):
    row_count = EPISODES * PREF
    base_key, col_key, row_key = jax.random.split(jax.random.fold_in(key, 101), 3)
    column_trend = 3.0 ** (jnp.arange(D, dtype=jnp.float32) / D)
    jitter = jnp.exp(jax.random.uniform(col_key, (D,), minval=-1.15, maxval=1.15))
    row_scale = jnp.exp(jax.random.uniform(row_key, (row_count, 1), minval=0.0, maxval=math.log(10.0)))
    base_draw = jnp.clip(jax.random.normal(base_key, (row_count, D)), -5.0, 5.0)
    return (base_draw * (column_trend * jitter)[None, :] * row_scale).astype(jnp.bfloat16)


def draw_action_states(key, part):
    row_count = EPISODES * ACT
    draw_key = jax.random.fold_in(jax.random.fold_in(key, 202), 0)
    base_draw = jnp.clip(jax.random.normal(draw_key, (EPISODES, ACT, DA)), -4.0, 4.0)
    return base_draw.reshape(row_count, DA).astype(jnp.bfloat16)


def draw_prefix_length(key, part):
    length_key, full_key = jax.random.split(jax.random.fold_in(key, 303))
    lengths = jax.random.randint(length_key, (EPISODES,), max(PREF // 4, 1), PREF + 1)
    full_slot = jax.random.randint(full_key, (), 0, EPISODES)
    return jnp.where(jnp.arange(EPISODES) == full_slot, PREF, lengths).astype(jnp.int32)


def draw_action_length(key, part):
    length_key, full_key = jax.random.split(jax.random.fold_in(key, 404))
    lengths = jax.random.randint(length_key, (EPISODES,), max(ACT // 4, 1), ACT + 1)
    full_slot = jax.random.randint(full_key, (), 0, EPISODES)
    return jnp.where(jnp.arange(EPISODES) == full_slot, ACT, lengths).astype(jnp.int32)


def block_scale(stream_key, shape, shards, smallest, largest):
    loudness, own = 1.0, jax.random.fold_in(stream_key, 6)
    for axis_at, shards_of in shards:
        heights = jnp.exp(jax.random.uniform(jax.random.fold_in(own, axis_at), (shards_of,), jnp.float32, smallest / len(shards), largest / len(shards)))
        loudness = loudness * jnp.repeat(heights, shape[axis_at] // shards_of).reshape([-1 if axis == axis_at else 1 for axis in range(len(shape))])
    return loudness


def bell_draw(stream_key, dims, scale, limit, cuts=(), held_as=jnp.bfloat16):
    values = jax.random.normal(stream_key, dims, jnp.float32) * scale
    if len(cuts) > 0:
        values = block_scale(stream_key, dims, cuts, -0.22, 0.18) * values
    return jnp.clip(values, min=-limit, max=limit).astype(held_as)


def setup_inputs(seed: int = 0, part: int = 0) -> dict:
    seeds = jax.random.split(jax.random.key(seed), 12)
    own_keys = jax.random.split(jax.random.fold_in(seeds[11], part), 12)
    return {
        "prefix_states": draw_prefix_states(jax.random.fold_in(jax.random.fold_in(seeds[11], part), 71), part),
        "prefix_gain": jnp.clip(1.0 + 0.18 * jax.random.normal(seeds[1], (D,), jnp.float32), 0.1, 1.9),
        "backbone_key": bell_draw(seeds[2], (D, KV), D ** -0.5, 0.0625, ((0, 8), (1, 2))),
        "backbone_value": bell_draw(seeds[3], (D, KV), D ** -0.5, 0.0625, ((0, 8), (1, 2))),
        "action_states": draw_action_states(jax.random.fold_in(jax.random.fold_in(seeds[11], part), 71), part),
        "expert_query": bell_draw(seeds[5], (DA, QW), (DA // 4) ** -0.5, 0.25, ((0, 8), (1, 2))),
        "expert_key": bell_draw(seeds[6], (DA, KV), DA ** -0.5, 0.125, ((0, 8), (1, 2))),
        "expert_value": bell_draw(seeds[7], (DA, KV), DA ** -0.5, 0.125, ((0, 8), (1, 2))),
        "expert_out": bell_draw(seeds[8], (QW, DA), (QW // 16) ** -0.5, 0.5, ((0, 2), (1, 8))),
        "prefix_length": draw_prefix_length(jax.random.fold_in(jax.random.fold_in(seeds[11], part), 71), part),
        "action_length": draw_action_length(jax.random.fold_in(jax.random.fold_in(seeds[11], part), 71), part),
    }


def attend(packed):
    prefix_k, prefix_v, query_e, key_e, value_e, prefix_valid, action_valid = packed
    queries = query_e.astype(jnp.float32).reshape(ACT, KV_HEADS, 2, HEAD)
    keys_all = jnp.concatenate([prefix_k, key_e], axis=0).astype(jnp.float32).reshape(PREF + ACT, KV_HEADS, HEAD)
    values_all = jnp.concatenate([prefix_v, value_e], axis=0).astype(jnp.float32).reshape(PREF + ACT, KV_HEADS, HEAD)
    valid = jnp.concatenate([jnp.arange(PREF) < prefix_valid, jnp.arange(ACT) < action_valid])
    scores = jnp.einsum('qgjd,kgd->gjqk', queries, keys_all) * HEAD ** (-0.5)
    scores = jnp.where(valid[None, None, None, :], scores, -1e+30)
    highest = lax.optimization_barrier(jnp.max(scores, axis=-1, keepdims=True))
    exponent = jnp.exp(scores - highest)
    weights = (exponent / lax.optimization_barrier(jnp.sum(exponent, axis=-1, keepdims=True))).astype(jnp.bfloat16)
    attended = jnp.einsum('gjqk,kgd->qgjd', weights.astype(jnp.float32), values_all)
    return attended.reshape(ACT, QW).astype(jnp.bfloat16)

def reference(prefix_states, prefix_gain, backbone_key, backbone_value, action_states, expert_query, expert_key, expert_value, expert_out, prefix_length, action_length):
    states = prefix_states.astype(jnp.float32)
    squares = lax.optimization_barrier(jnp.sum(states * states, axis=1, keepdims=True))
    normed = (states * lax.rsqrt(squares / D + 1e-06) * prefix_gain[None, :]).astype(jnp.bfloat16)
    prefix_keys = jnp.dot(normed, backbone_key, preferred_element_type=jnp.float32).astype(jnp.bfloat16)
    prefix_values = jnp.dot(normed, backbone_value, preferred_element_type=jnp.float32).astype(jnp.bfloat16)
    action_query = jnp.dot(action_states, expert_query, preferred_element_type=jnp.float32).astype(jnp.bfloat16)
    action_key = jnp.dot(action_states, expert_key, preferred_element_type=jnp.float32).astype(jnp.bfloat16)
    action_value = jnp.dot(action_states, expert_value, preferred_element_type=jnp.float32).astype(jnp.bfloat16)
    packed = (prefix_keys.reshape(EPISODES, PREF, KV), prefix_values.reshape(EPISODES, PREF, KV), action_query.reshape(EPISODES, ACT, QW), action_key.reshape(EPISODES, ACT, KV), action_value.reshape(EPISODES, ACT, KV), prefix_length, action_length)
    attended = lax.map(attend, packed).reshape(EPISODES * ACT, QW)
    action_out = jnp.dot(attended, expert_out, preferred_element_type=jnp.float32).astype(jnp.bfloat16)
    return (prefix_keys, prefix_values, action_out)
```

```python
import functools

import jax
import jax.numpy as jnp
from jax import lax
from jax.experimental import pallas as pl
from jax.experimental.pallas import tpu as pltpu
from jax.sharding import PartitionSpec as P

D = 8192
HEAD = 128
LOG2E = 1.4426950408889634


f32 = jnp.float32
bf16 = jnp.bfloat16
ANY = pl.BlockSpec(memory_space=pl.ANY)


def ring_order(count):
    return list(range(0, count, 2)) + list(range(count - 1, 0, -2))


def ring_pairs(count, step):
    order = ring_order(count)
    return [(order[i], order[(i + step) % count]) for i in range(count)]


def ring_table(count):
    order = ring_order(count)
    half = count // 2
    rows = [None] * count
    for place, device in enumerate(order):
        behind = [order[(place - k) % count] for k in range(1, half + 1)]
        ahead = [order[(place + k) % count] for k in range(1, half)]
        rows[device] = [device] + behind + ahead
    return jnp.array(rows, jnp.int32)


def ring_gather(block, count, first, second):
    half = count // 2
    up, down = ring_pairs(count, 1), ring_pairs(count, -1)
    behind, ahead = [block], [block]
    for _ in range(half - 1):
        behind.append(lax.ppermute(behind[-1], "row", up))
        ahead.append(lax.ppermute(ahead[-1], "row", down))
    far_first = lax.ppermute(first(behind[-1]), "row", up)
    far_second = lax.ppermute(second(ahead[-1]), "row", down)
    return behind[1:], ahead[1:], far_first, far_second


def prefix_kernel(place, mine, other, gain, key_w, value_w, out):
    block = pl.program_id(0)
    per_half = pl.num_programs(0) // 2
    is_mine = block // per_half == place[0]
    states = jnp.where(is_mine, mine[...], other[...]).astype(f32)
    squares = jnp.sum(states * states, axis=1, keepdims=True)
    scaled = (states * gain[...]).astype(bf16)
    cols = key_w.shape[1]
    out[:, :cols] = jnp.dot(scaled, key_w[...], preferred_element_type=f32)
    out[:, cols : 2 * cols] = jnp.dot(scaled, value_w[...], preferred_element_type=f32)
    out[:, 2 * cols :] = jnp.broadcast_to(squares, (squares.shape[0], HEAD))


def prefix_partial(col, mine, other, gain, key_w, value_w, rows):
    half_tokens, features = mine.shape
    block = 2 * half_tokens // rows
    per_half = rows // 2
    cols = key_w.shape[1]
    return pl.pallas_call(
        prefix_kernel,
        grid_spec=pltpu.PrefetchScalarGridSpec(
            num_scalar_prefetch=1,
            grid=(rows,),
            in_specs=[
                pl.BlockSpec((block, features), lambda i, p: (i % per_half, 0)),
                pl.BlockSpec((block, features), lambda i, p: (i % per_half, 0)),
                pl.BlockSpec((1, features), lambda i, p: (0, 0)),
                pl.BlockSpec((features, cols), lambda i, p: (0, 0)),
                pl.BlockSpec((features, cols), lambda i, p: (0, 0)),
            ],
            out_specs=pl.BlockSpec((block, 2 * cols + HEAD), lambda i, p: (i, 0)),
        ),
        out_shape=jax.ShapeDtypeStruct((2 * half_tokens, 2 * cols + HEAD), f32),
        name="prefix_partial",
    )(col.reshape(1), mine, other, gain.reshape(1, -1), key_w, value_w)


def project_kernel(count, place, owners, mine, other, *refs):
    half = count // 2
    own = refs[:3]
    pieces = refs[3 : 3 + count - 2]
    far_first, far_second = refs[3 + count - 2 : 3 + count]
    query_out, key_out, value_out, weights, sems = refs[3 + count :]
    step = pl.program_id(0)
    rows, query_cols = own[0].shape
    kv_cols = own[1].shape[1]
    features = weights.shape[0]
    half_features = features // 2
    starts = [0, query_cols, query_cols + kv_cols, query_cols + 2 * kv_cols]

    def position(owner):
        at = owner * rows + features - place[0] * half_features
        return pl.multiple_of(lax.rem(at, features), rows)

    def copies():
        out = [[], [], []]
        at = position(owners[0])
        for j in range(3):
            out[j].append(
                pltpu.make_async_copy(
                    own[j],
                    weights.at[pl.ds(at, rows), starts[j] : starts[j + 1]],
                    sems.at[j, 0],
                )
            )
        for i in range(count - 2):
            index = 1 + i if i < half - 1 else 2 + i
            at = position(owners[index])
            for j in range(3):
                out[j].append(
                    pltpu.make_async_copy(
                        pieces[i].at[:, starts[j] : starts[j + 1]],
                        weights.at[pl.ds(at, rows), starts[j] : starts[j + 1]],
                        sems.at[j, 1 + i],
                    )
                )
        at = position(owners[half])
        for j in range(3):
            ref, base = (far_first, 0) if j == 0 else (far_second, query_cols)
            out[j].append(
                pltpu.make_async_copy(
                    ref.at[:, starts[j] - base : starts[j + 1] - base],
                    weights.at[pl.ds(at, rows), starts[j] : starts[j + 1]],
                    sems.at[j, count - 1],
                )
            )
        return out

    scale = HEAD**-0.5 * LOG2E

    def total(j):
        cols = slice(starts[j], starts[j + 1])
        return jnp.dot(
            mine[...], weights[:half_features, cols], preferred_element_type=f32
        ) + jnp.dot(other[...], weights[half_features:, cols], preferred_element_type=f32)

    @pl.when(step == 0)
    def _():
        groups = copies()
        for j in (1, 2, 0):
            for copy in groups[j]:
                copy.start()
        for j in (1, 2, 0):
            for copy in groups[j]:
                copy.wait()

    key_out[...] = total(1).astype(bf16)
    value_out[...] = total(2).astype(bf16)
    query_out[...] = (total(0) * scale).astype(bf16)


def project(col, owners, mine, other, own, pieces, far, count):
    tokens, half_features = mine.shape
    query_cols, kv_cols = own[0].shape[1], own[1].shape[1]
    tile = min(256, tokens)
    row = lambda i, *_: (i, 0)
    return pl.pallas_call(
        functools.partial(project_kernel, count),
        grid_spec=pltpu.PrefetchScalarGridSpec(
            num_scalar_prefetch=2,
            grid=(tokens // tile,),
            in_specs=[pl.BlockSpec((tile, half_features), row)] * 2 + [ANY] * (3 + count),
            out_specs=[
                pl.BlockSpec((tile, query_cols), row),
                pl.BlockSpec((tile, kv_cols), row),
                pl.BlockSpec((tile, kv_cols), row),
            ],
            scratch_shapes=[
                pltpu.VMEM((2 * half_features, query_cols + 2 * kv_cols), bf16),
                pltpu.SemaphoreType.DMA((3, count)),
            ],
        ),
        out_shape=[
            jax.ShapeDtypeStruct((tokens, query_cols), bf16),
            jax.ShapeDtypeStruct((tokens, kv_cols), bf16),
            jax.ShapeDtypeStruct((tokens, kv_cols), bf16),
        ],
        name="project",
    )(col.reshape(1), owners, mine, other, *own, *pieces, *far)


def attend_kernel(lengths, query, key, value, prefix_key, prefix_value, out, keys, values):
    prefix_count = prefix_key.shape[0]
    count = key.shape[0]
    total = prefix_count + count

    @pl.when(pl.program_id(1) == 0)
    def _():
        keys[:count, :HEAD] = key[...]
        keys[count:, :HEAD] = prefix_key[...]
        at = lax.broadcasted_iota(jnp.int32, (total, HEAD), 0)
        lane = lax.broadcasted_iota(jnp.int32, (total, HEAD), 1)
        limit = jnp.where(at < count, lengths[1], lengths[0] + count)
        keys[:, HEAD:] = jnp.where((at >= limit) & (lane == 0), -1e30, 0.0).astype(bf16)
        values[:count, :HEAD] = value[...]
        values[count:, :HEAD] = prefix_value[...]
        values[:, HEAD:] = jnp.ones((total, HEAD), bf16)

    ones = jnp.ones((query.shape[0], HEAD), bf16)
    for j in range(2):
        wide = jnp.concatenate([query[:, j * HEAD : (j + 1) * HEAD], ones], axis=1)
        scores = lax.dot_general(
            wide, keys[...], (((1,), (1,)), ((), ())), preferred_element_type=f32
        )
        highest = jnp.max(scores, axis=1, keepdims=True)
        weights = jnp.exp2(scores - highest).astype(bf16)
        both = jnp.dot(weights, values[...], preferred_element_type=f32)
        out[:, j * HEAD : (j + 1) * HEAD] = (both[:, :HEAD] / both[:, HEAD:]).astype(bf16)


def attend(lengths, query, key, value, prefix_key, prefix_value, first, groups):
    tokens = query.shape[0]
    prefix_count = prefix_key.shape[0]
    tile = min(256, tokens)
    total = tokens + prefix_count
    return pl.pallas_call(
        attend_kernel,
        grid_spec=pltpu.PrefetchScalarGridSpec(
            num_scalar_prefetch=1,
            grid=(groups, tokens // tile),
            in_specs=[
                pl.BlockSpec((tile, 2 * HEAD), lambda g, i, p: (i, first + g)),
                pl.BlockSpec((tokens, HEAD), lambda g, i, p: (0, first + g)),
                pl.BlockSpec((tokens, HEAD), lambda g, i, p: (0, first + g)),
                pl.BlockSpec((prefix_count, HEAD), lambda g, i, p: (0, first + g)),
                pl.BlockSpec((prefix_count, HEAD), lambda g, i, p: (0, first + g)),
            ],
            out_specs=pl.BlockSpec((tile, 2 * HEAD), lambda g, i, p: (i, g)),
            scratch_shapes=[
                pltpu.VMEM((total, 2 * HEAD), bf16),
                pltpu.VMEM((total, 2 * HEAD), bf16),
            ],
        ),
        out_shape=jax.ShapeDtypeStruct((tokens, groups * 2 * HEAD), bf16),
        name="attend",
    )(lengths, query, key, value, prefix_key, prefix_value)


def out_kernel(count, parts, side, place, owners, *refs):
    half = count // 2
    attended = refs[:parts]
    own = refs[parts]
    pieces = refs[parts + 1 : parts + 1 + count - 2]
    far_first, far_second = refs[parts + count - 1 : parts + 1 + count]
    out, weights, sems = refs[parts + 1 + count :]
    rows, cols = own.shape
    near = half * cols

    @pl.when(pl.program_id(0) == 0)
    def _():
        def copies():
            todo = [(own, 0, 0, rows)]
            for i in range(count - 2):
                todo.append((pieces[i], 1 + i if i < half - 1 else 2 + i, 0, rows))
            todo.append((far_first, half, 0, rows // 2))
            todo.append((far_second, half, rows // 2, rows))
            for at, (ref, index, low, high) in enumerate(todo):
                owner = owners[index]
                here = jnp.where(place[0] == side, owner // half == 0, owner // half == 1)
                to = pl.multiple_of(lax.rem(owner, half) * cols, cols)
                yield here, pltpu.make_async_copy(
                    ref, weights.at[low:high, pl.ds(to, cols)], sems.at[at]
                )

        for here, copy in copies():
            pl.when(here)(copy.start)
        for here, copy in copies():
            pl.when(here)(copy.wait)

    depth = rows // parts
    total = jnp.dot(attended[0][...], weights[:depth], preferred_element_type=f32)
    for j in range(1, parts):
        total += jnp.dot(
            attended[j][...], weights[j * depth : (j + 1) * depth], preferred_element_type=f32
        )
    out[...] = total.astype(out.dtype)


def project_out(col, owners, attended, own, pieces, far, count, side, dtype):
    tokens = attended[0].shape[0]
    rows, cols = own.shape
    tile = min(256, tokens)
    width = count // 2 * cols
    parts = len(attended)
    return pl.pallas_call(
        functools.partial(out_kernel, count, parts, side),
        grid_spec=pltpu.PrefetchScalarGridSpec(
            num_scalar_prefetch=2,
            grid=(tokens // tile,),
            in_specs=[pl.BlockSpec((tile, rows // parts), lambda i, *_: (i, 0))] * parts
            + [ANY] * (1 + count),
            out_specs=pl.BlockSpec((tile, width), lambda i, *_: (i, 0)),
            scratch_shapes=[
                pltpu.VMEM((rows, width), bf16),
                pltpu.SemaphoreType.DMA((count + 1,)),
            ],
        ),
        out_shape=jax.ShapeDtypeStruct((tokens, width), dtype),
        name="project_out",
    )(col.reshape(1), owners, *attended, own, *pieces, *far)


def reduce_ring(partial, table, count):
    half = count // 2
    up, down = ring_pairs(count, 1), ring_pairs(count, -1)
    block = partial.shape[0] // count
    cols = (partial.shape[1] - HEAD) // 2

    def part(owner):
        return lax.dynamic_slice_in_dim(partial, owner * block, block, 0)

    def pack(total):
        squares = total[:, 2 * cols :]
        high = squares.astype(bf16)
        low = (squares - high.astype(f32)).astype(bf16)
        lane = lax.broadcasted_iota(jnp.int32, squares.shape, 1)
        return jnp.concatenate(
            [total[:, : 2 * cols].astype(bf16), jnp.where(lane < HEAD // 2, high, low)], axis=1
        )

    def unpack(message):
        tail = message[:, -HEAD:].astype(f32)
        squares = tail[:, :1] + tail[:, HEAD // 2 : HEAD // 2 + 1]
        return jnp.concatenate(
            [message[:, :-HEAD].astype(f32), jnp.broadcast_to(squares, tail.shape)], axis=1
        )

    far = pack(part(table[half]))
    send_up, send_down = far[:, :cols], far[:, cols:]
    for k in range(half - 1, 0, -1):
        got_up = lax.ppermute(send_up, "row", up)
        got_down = lax.ppermute(send_down, "row", down)
        mine_up, mine_down = part(table[half + k]), part(table[k])
        if k == half - 1:
            total_up = jnp.concatenate(
                [mine_up[:, :cols] + got_up.astype(f32), mine_up[:, cols:]], axis=1
            )
            total_down = jnp.concatenate(
                [mine_down[:, :cols], mine_down[:, cols:] + unpack(got_down)], axis=1
            )
        else:
            total_up = mine_up + unpack(got_up)
            total_down = mine_down + unpack(got_down)
        send_up, send_down = pack(total_up), pack(total_down)
    got_up = lax.ppermute(send_up, "row", up)
    got_down = lax.ppermute(send_down, "row", down)
    mine = part(table[0])
    return mine + unpack(got_up) + unpack(got_down)


def shards(
    rows,
    prefix_states,
    prefix_gain,
    backbone_key,
    backbone_value,
    action_states,
    expert_query,
    expert_key,
    expert_value,
    expert_out,
    prefix_length,
    action_length,
):
    swap = [(0, 1), (1, 0)]
    col = lax.axis_index("col").astype(jnp.int32)
    table = ring_table(rows)[lax.axis_index("row")]
    key_cols = backbone_key.shape[1]
    query_cols = expert_query.shape[1]

    other_states = lax.ppermute(prefix_states, "col", swap)
    other_actions = lax.ppermute(action_states, "col", swap)

    joined = jnp.concatenate([expert_query, expert_key, expert_value], axis=1)
    behind, ahead, far_first, far_second = ring_gather(
        joined, rows, lambda b: b[:, :query_cols], lambda b: b[:, query_cols:]
    )

    partial = prefix_partial(
        col, prefix_states, other_states, prefix_gain, backbone_key, backbone_value, rows
    )
    total = reduce_ring(partial, table, rows)
    scale = lax.rsqrt(total[:, 2 * key_cols :][:, :1] / D + 1e-06)
    prefix_keys = (total[:, :key_cols] * scale).astype(bf16)
    prefix_values = (total[:, key_cols : 2 * key_cols] * scale).astype(bf16)

    query, key, value = project(
        col,
        table,
        action_states,
        other_actions,
        (expert_query, expert_key, expert_value),
        behind + ahead,
        (far_first, far_second),
        rows,
    )

    out_rows = expert_out.shape[0] // 2
    out_behind, out_ahead, out_first, out_second = ring_gather(
        expert_out, rows, lambda b: b[:out_rows], lambda b: b[out_rows:]
    )

    lengths = jnp.concatenate([prefix_length, action_length])
    groups = key.shape[1] // HEAD
    attended = [
        attend(lengths, query, key, value, prefix_keys, prefix_values, g, 1) for g in range(groups)
    ]

    def outward(side, dtype):
        return project_out(
            col,
            table,
            attended,
            expert_out,
            out_behind + out_ahead,
            (out_first, out_second),
            rows,
            side,
            dtype,
        )

    given = outward(1, bf16)
    got = lax.ppermute(given, "col", swap)
    kept = outward(0, f32)
    action_out = (kept + got.astype(f32)).astype(bf16)
    return (prefix_keys, prefix_values, action_out)


def solution(mesh):
    placed = (
        P(("groups", "col"), "row"),
        P("row"),
        P("row", "col"),
        P("row", "col"),
        P(("groups", "row"), "col"),
        P("row", "col"),
        P("row", "col"),
        P("row", "col"),
        P("col", "row"),
        P(("groups", "row")),
        P(("groups", "row")),
    )
    return jax.shard_map(
        functools.partial(shards, mesh.shape["row"]),
        mesh=mesh,
        in_specs=placed,
        out_specs=(
            P(("groups", "row"), "col"),
            P(("groups", "row"), "col"),
            P(("groups", "row"), "col"),
        ),
        check_vma=False,
    )
```

```python
import functools

import jax
import jax.numpy as jnp
from jax import lax
from jax.experimental import pallas as pl
from jax.experimental.pallas import tpu as pltpu
from jax.sharding import PartitionSpec as P


D = 8192
HEAD = 128
LOG2E = 1.4426950408889634


f32 = jnp.float32
bf16 = jnp.bfloat16
ANY = pl.BlockSpec(memory_space=pl.ANY)


def ring_order(count):
    return list(range(0, count, 2)) + list(range(count - 1, 0, -2))


def ring_pairs(count, step):
    order = ring_order(count)
    return [(order[i], order[(i + step) % count]) for i in range(count)]


def spot_of(replicas):
    at = lax.axis_index("row") * 2 + lax.axis_index("col")
    return (at * replicas + lax.axis_index("groups")).astype(jnp.int32).reshape(1)


class Spot:
    def __init__(self, count, replicas, value):
        self.count = count
        self.group = lax.rem(value, replicas)
        self.col = lax.rem(lax.div(value, replicas), 2)
        self.row = lax.div(value, 2 * replicas)

    def owner(self, entry):
        count = self.count
        half = count // 2
        low = lax.div(self.row, 2)
        place = jnp.where(lax.rem(self.row, 2) == 0, low, count - 1 - low)
        place = lax.rem(place + (count - entry if entry <= half else entry - half), count)
        return jnp.where(place < half, 2 * place, 2 * (count - 1 - place) + 1)


def prefix_kernel(spot, at, mine, other, gain, key_w, value_w, out):
    per_half = pl.num_programs(0) // 2
    is_mine = pl.program_id(0) // per_half == spot(at[0]).col
    states = jnp.where(is_mine, mine[...], other[...]).astype(f32)
    squares = jnp.sum(states * states, axis=1, keepdims=True)
    scaled = (states * gain[...]).astype(bf16)
    cols = key_w.shape[1]
    out[:, :cols] = jnp.dot(scaled, key_w[...], preferred_element_type=f32).astype(bf16)
    out[:, cols : 2 * cols] = jnp.dot(scaled, value_w[...], preferred_element_type=f32).astype(bf16)
    out[:, 2 * cols :] = packed(squares)


def prefix_partial(spot, at, mine, other, gain, key_w, value_w):
    half_tokens, features = mine.shape
    tile = min(256, half_tokens)
    per_half = half_tokens // tile
    cols = key_w.shape[1]
    same = lambda i, p: (0, 0)
    return pl.pallas_call(
        functools.partial(prefix_kernel, spot),
        grid_spec=pltpu.PrefetchScalarGridSpec(
            num_scalar_prefetch=1,
            grid=(2 * per_half,),
            in_specs=[
                pl.BlockSpec((tile, features), lambda i, p: (i % per_half, 0)),
                pl.BlockSpec((tile, features), lambda i, p: (i % per_half, 0)),
                pl.BlockSpec((1, features), same),
                pl.BlockSpec((features, cols), same),
                pl.BlockSpec((features, cols), same),
            ],
            out_specs=pl.BlockSpec((tile, 2 * cols + HEAD), lambda i, p: (i, 0)),
        ),
        out_shape=jax.ShapeDtypeStruct((2 * half_tokens, 2 * cols + HEAD), bf16),
        compiler_params=pltpu.CompilerParams(vmem_limit_bytes=16 << 20),
        name="prefix_partial",
    )(at, mine, other, gain.reshape(1, -1), key_w, value_w)


def packed(squares):
    high = squares.astype(bf16)
    low = (squares - high.astype(f32)).astype(bf16)
    shape = (squares.shape[0], HEAD)
    lane = lax.broadcasted_iota(jnp.int32, shape, 1)
    return jnp.where(
        lane < HEAD // 2,
        jnp.broadcast_to(high.astype(f32), shape),
        jnp.broadcast_to(low.astype(f32), shape),
    ).astype(bf16)


def squares_of(tail):
    wide = tail.astype(f32)
    return wide[:, :1] + wide[:, HEAD // 2 : HEAD // 2 + 1]


def reduce_step_kernel(at, block_up, block_down, got_up, got_down, up, down):
    full = up.shape[1] - HEAD
    for block, got, out in ((block_up, got_up, up), (block_down, got_down, down)):
        width = got.shape[1]
        if width == full // 2:
            low, high = 0, width
        elif width == full // 2 + HEAD:
            low, high = full // 2, full
        else:
            low, high = 0, full
        if low > 0:
            out[:, :low] = block[:, :low]
        total = block[:, low:high].astype(f32) + got[:, : high - low].astype(f32)
        out[:, low:high] = total.astype(bf16)
        if high < full:
            out[:, high:] = block[:, high:]
        else:
            out[:, full:] = packed(squares_of(block[:, full:]) + squares_of(got[:, high - low :]))


def reduce_last_kernel(at, block, got_up, got_down, keys, values, keys_too, values_too):
    cols = keys.shape[1]
    total = block[:, : 2 * cols].astype(f32) + got_up[:, : 2 * cols].astype(f32)
    total = total + got_down[:, : 2 * cols].astype(f32)
    squares = squares_of(block[:, 2 * cols :])
    squares = squares + squares_of(got_up[:, 2 * cols :]) + squares_of(got_down[:, 2 * cols :])
    total = total * lax.rsqrt(squares / D + 1e-06)
    for out in (keys, keys_too):
        out[...] = total[:, :cols].astype(bf16)
    for out in (values, values_too):
        out[...] = total[:, cols:].astype(bf16)


def reduce_call(kernel, spot, at, partial, block, places, got, widths):
    whole = lambda a: pl.BlockSpec(a, lambda i, t: (0, 0))
    taken = [
        pl.BlockSpec((block, partial.shape[1]), functools.partial(lambda n, i, t: (spot(t[0]).owner(n), 0), n))
        for n in places
    ]
    return pl.pallas_call(
        kernel,
        grid_spec=pltpu.PrefetchScalarGridSpec(
            num_scalar_prefetch=1,
            grid=(1,),
            in_specs=taken + [whole(g.shape) for g in got],
            out_specs=[whole((block, w)) for w in widths],
        ),
        out_shape=[jax.ShapeDtypeStruct((block, w), bf16) for w in widths],
        compiler_params=pltpu.CompilerParams(vmem_limit_bytes=8 << 20),
    )(at, *[partial] * len(places), *got)


class Plan:
    def __init__(self, rows, width, segments):
        self.rows, self.width, self.segments = rows, width, segments
        self.copies, self.refs = [], []

    def add(self, array, low, count, entry, segment, offset=0, group=None):
        for at, known in enumerate(self.refs):
            if known is array:
                break
        else:
            at = len(self.refs)
            self.refs.append(array)
        self.copies.append((at, low, count, entry, segment, offset, group))


def project_kernel(plan, scale, spot, at, mine, other, *refs):
    sources = refs[: len(plan.refs)]
    *outs, weights, sems = refs[len(plan.refs) :]
    rows, width = plan.rows, plan.width
    half_features = mine.shape[1]
    features = 2 * half_features
    here = spot(at[0])

    def copies(segment):
        for index, (ref, low, count, entry, to, offset, group) in enumerate(plan.copies):
            if to != segment:
                continue
            row = here.owner(entry) * rows + features - here.col * half_features
            row = lax.rem(row, features)
            row = row + offset
            if group is not None:
                row = row + (here.group if group == 0 else 1 - here.group) * count
            source = sources[ref]
            col = to * width if source.shape[1] > width else 0
            yield pltpu.make_async_copy(
                source.at[low : low + count, col : col + width],
                weights.at[
                    pl.ds(pl.multiple_of(row, count), count), to * width : (to + 1) * width
                ],
                sems.at[index],
            )

    for segment in range(plan.segments):
        for copy in copies(segment):
            copy.start()
    for segment in range(plan.segments):
        for copy in copies(segment):
            copy.wait()
        cols = slice(segment * width, (segment + 1) * width)
        total = jnp.dot(mine[...], weights[:half_features, cols], preferred_element_type=f32)
        total += jnp.dot(other[...], weights[half_features:, cols], preferred_element_type=f32)
        if scale is not None:
            total = total * scale
        if len(outs) == plan.segments:
            outs[segment][...] = total.astype(bf16)
        else:
            outs[0][:, cols] = total.astype(bf16)


def project(spot, at, mine, other, plan, widths, scale=None):
    tokens, half_features = mine.shape
    row = lambda i, *_: (i, 0)
    return pl.pallas_call(
        functools.partial(project_kernel, plan, scale, spot),
        grid_spec=pltpu.PrefetchScalarGridSpec(
            num_scalar_prefetch=1,
            grid=(1,),
            in_specs=[pl.BlockSpec((tokens, half_features), row)] * 2 + [ANY] * len(plan.refs),
            out_specs=[pl.BlockSpec((tokens, w), row) for w in widths],
            scratch_shapes=[
                pltpu.VMEM((2 * half_features, plan.segments * plan.width), bf16),
                pltpu.SemaphoreType.DMA((len(plan.copies),)),
            ],
        ),
        out_shape=[jax.ShapeDtypeStruct((tokens, w), bf16) for w in widths],
        compiler_params=pltpu.CompilerParams(vmem_limit_bytes=24 << 20),
        name="project",
    )(at, mine, other, *plan.refs)


def attend_kernel(prefix_length, action_length, query, key, value, prefix_key, prefix_value, out, keys, values):
    prefix_count = prefix_key.shape[0]
    count = key.shape[0]
    total = prefix_count + count
    tile = min(256, query.shape[0])

    keys[:count, :HEAD] = key[...]
    keys[count:, :HEAD] = prefix_key[...]
    at = lax.broadcasted_iota(jnp.int32, (total, HEAD), 0)
    lane = lax.broadcasted_iota(jnp.int32, (total, HEAD), 1)
    limit = jnp.where(at < count, action_length[0], prefix_length[0] + count)
    keys[:, HEAD:] = jnp.where((at >= limit) & (lane == 0), -1e30, 0.0).astype(bf16)
    values[:count, :HEAD] = value[...]
    values[count:, :HEAD] = prefix_value[...]
    values[:, HEAD:] = jnp.ones((total, HEAD), bf16)
    ones = jnp.ones((tile, HEAD), bf16)

    def place(unit):
        head, at = unit
        return slice(at * tile, (at + 1) * tile), slice(head * HEAD, (head + 1) * HEAD)

    def score(unit):
        wide = jnp.concatenate([query[place(unit)], ones], axis=1)
        return lax.dot_general(
            wide, keys[...], (((1,), (1,)), ((), ())), preferred_element_type=f32
        )

    units = [(head, at) for at in range(query.shape[0] // tile) for head in range(2)]
    following = score(units[0])
    for index, unit in enumerate(units):
        scores = following
        if index + 1 < len(units):
            following = score(units[index + 1])
        highest = jnp.max(scores, axis=1, keepdims=True)
        weights = jnp.exp2(scores - highest).astype(bf16)
        both = jnp.dot(weights, values[...], preferred_element_type=f32)
        out[place(unit)] = (both[:, :HEAD] / both[:, HEAD:]).astype(bf16)


def attend(prefix_length, action_length, query, key, value, prefix_key, prefix_value, first, groups):
    tokens = query.shape[0]
    prefix_count = prefix_key.shape[0]
    total = tokens + prefix_count
    at = lambda g, *_: (0, first + g)
    return pl.pallas_call(
        attend_kernel,
        grid_spec=pltpu.PrefetchScalarGridSpec(
            num_scalar_prefetch=2,
            grid=(groups,),
            in_specs=[
                pl.BlockSpec((tokens, 2 * HEAD), at),
                pl.BlockSpec((tokens, HEAD), at),
                pl.BlockSpec((tokens, HEAD), at),
                pl.BlockSpec((prefix_count, HEAD), at),
                pl.BlockSpec((prefix_count, HEAD), at),
            ],
            out_specs=pl.BlockSpec((tokens, 2 * HEAD), lambda g, *_: (0, g)),
            scratch_shapes=[
                pltpu.VMEM((total, 2 * HEAD), bf16),
                pltpu.VMEM((total, 2 * HEAD), bf16),
            ],
        ),
        out_shape=jax.ShapeDtypeStruct((tokens, groups * 2 * HEAD), bf16),
        compiler_params=pltpu.CompilerParams(vmem_limit_bytes=16 << 20),
        name="attend",
    )(prefix_length, action_length, query, key, value, prefix_key, prefix_value)


def out_kernel(plan, side, parts, spot, at, *refs):
    place = spot(at[0])
    attended = refs[:parts]
    sources = refs[parts : parts + len(plan.refs)]
    got = refs[parts + len(plan.refs) : -3]
    out, weights, sems = refs[-3:]
    rows, cols = weights.shape[0], plan.width
    half = weights.shape[1] // cols
    quarter = rows // 4
    first = pl.program_id(0) == 0

    @pl.when(first)
    def _():
        for ref, low, count, entry, _, offset, group in plan.copies:
            owner = place.owner(entry)
            to = lax.rem(owner, half)
            mine = owner // half == place.col
            here = mine if side == 0 else jnp.logical_not(mine)
            first_quarter = offset // quarter
            if group is not None:
                first_quarter += 2 * (place.group if group == 0 else 1 - place.group)

            @pl.when(here)
            def _():
                for i in range(count // quarter):
                    row = pl.multiple_of((first_quarter + i) * quarter, quarter)
                    pltpu.make_async_copy(
                        sources[ref].at[low + i * quarter : low + (i + 1) * quarter],
                        weights.at[
                            pl.ds(row, quarter), pl.ds(pl.multiple_of(to * cols, cols), cols)
                        ],
                        sems.at[first_quarter + i, to],
                    ).start()

        for to in range(half):
            for i in range(4):
                pltpu.make_async_copy(
                    sources[0].at[:quarter],
                    weights.at[i * quarter : (i + 1) * quarter, to * cols : (to + 1) * cols],
                    sems.at[i, to],
                ).wait()

    depth = rows // parts
    total = jnp.dot(attended[0][...], weights[:depth], preferred_element_type=f32)
    for j in range(1, parts):
        total += jnp.dot(
            attended[j][...], weights[j * depth : (j + 1) * depth], preferred_element_type=f32
        )
    if len(got) == 1:
        total += got[0][...].astype(f32)
    elif len(got) == 2:
        early = pl.program_id(0) < pl.num_programs(0) - 1
        total += jnp.where(early, got[0][...], got[1][...]).astype(f32)
    out[...] = total.astype(out.dtype)


def project_out(spot, at, attended, plan, rows, half, got, start, size, side, dtype):
    tile = min(512, size)
    width = half * plan.width
    parts = len(attended)
    args = [at, *attended, *plan.refs, *got]
    specs = [pl.BlockSpec((tile, rows // parts), lambda i, *_: (i + start // tile, 0))] * parts
    specs += [ANY] * len(plan.refs)
    for array in got:
        last = array.shape[0] // tile - 1
        specs.append(
            pl.BlockSpec(
                (tile, width), functools.partial(lambda n, i, *_: (jnp.minimum(i, n), 0), last)
            )
        )
    return pl.pallas_call(
        functools.partial(out_kernel, plan, side, parts, spot),
        grid_spec=pltpu.PrefetchScalarGridSpec(
            num_scalar_prefetch=1,
            grid=(size // tile,),
            in_specs=specs,
            out_specs=pl.BlockSpec((tile, width), lambda i, *_: (i, 0)),
            scratch_shapes=[
                pltpu.VMEM((rows, width), bf16),
                pltpu.SemaphoreType.DMA((4, half)),
            ],
        ),
        out_shape=pltpu.VMEM((size, width), f32)
        if side == 0
        else jax.ShapeDtypeStruct((size, width), dtype),
        compiler_params=pltpu.CompilerParams(vmem_limit_bytes=24 << 20),
        name="project_out",
    )(*args)


def shards(
    count,
    replicas,
    prefix_states,
    prefix_gain,
    backbone_key,
    backbone_value,
    action_states,
    expert_query,
    expert_key,
    expert_value,
    expert_out,
    prefix_length,
    action_length,
):
    half = count // 2
    up, down = ring_pairs(count, 1), ring_pairs(count, -1)
    swap = [(0, 1), (1, 0)]
    spot = functools.partial(Spot, count, replicas)
    at = spot_of(replicas)
    rows, width = expert_key.shape
    query_cols = expert_query.shape[1]
    out_rows, out_cols = expert_out.shape

    shared = shares(replicas, rows)
    part = rows // 2 if shared else rows
    group = 0 if shared else None

    def own_half(array, low, width):
        if shared:
            return lax.dynamic_slice(array, (lax.axis_index("groups") * part, low), (part, width))
        return array[:, low : low + width]

    def around(pair):
        return [lax.ppermute(pair[0], "row", up), lax.ppermute(pair[1], "row", down)]

    def across(pair):
        joined = jnp.concatenate(pair, axis=0) if len(pair) > 1 else pair[0]
        joined = lax.ppermute(joined, "groups", swap)
        return [(joined, i * a.shape[0]) for i, a in enumerate(pair)]

    def ring(block, cut):
        pair = [block, block]
        for k in range(1, half + 1):
            if k == half:
                pair = [pair[0][:cut], pair[1][cut:]]
            pair = around(pair)
            yield k, pair, (k, half + k if k < half else half)

    strips = query_cols // width
    kv_plan, query_plan = Plan(rows, width, 2), Plan(rows, width, strips)
    kv_plan.add(expert_key, 0, rows, 0, 0)
    kv_plan.add(expert_value, 0, rows, 0, 1)
    for segment in range(strips):
        query_plan.add(expert_query, 0, rows, 0, segment)
    cut = (strips - 1) * part
    pair = jnp.concatenate([own_half(expert_key, 0, width), own_half(expert_value, 0, width)], axis=0)
    pair = [pair, pair]
    rest = [own_half(expert_query, i * width, width) for i in range(strips - 1)]
    rest = jnp.concatenate([*rest, expert_query[:, (strips - 1) * width :]], axis=0)
    rest = [rest, rest]
    for k in range(1, half + 1):
        entries = [k, half + k] if k < half else [half, half]
        if k == half:
            pair, rest = [pair[0][:part], pair[1][part:]], [rest[0][:cut], rest[1][cut:]]
        pair, rest = around(pair), around(rest)
        crossed = across(pair) if shared else []
        for side, arrays in ((group, [(a, 0) for a in pair]), (1, crossed)):
            for i, ((array, base), entry) in enumerate(zip(arrays, entries)):
                for segment in range(2) if k < half else [i]:
                    low = base + (segment * part if k < half else 0)
                    kv_plan.add(array, low, part, entry, segment, 0, side)
        split = [r[:cut] for r in rest] if k < half else rest[:1]
        crossed = across(split) if shared else []
        arrays = [(a, 0) for a in (rest if k < half else rest[:1])]
        for side, arrays in ((group, arrays), (1, crossed)):
            for (array, base), entry in zip(arrays, entries):
                for segment in range(strips - 1):
                    query_plan.add(array, base + segment * part, part, entry, segment, 0, side)
        for array, entry in zip(rest if k < half else rest[1:], entries):
            query_plan.add(array, cut if k < half else 0, rows, entry, strips - 1)

    out_plan = Plan(out_rows, out_cols, 1)
    out_plan.add(expert_out, 0, out_rows, 0, 0)
    out_part = out_rows // 2 if shared else out_rows
    message = expert_out
    if shared:
        message = lax.dynamic_slice_in_dim(expert_out, lax.axis_index("groups") * out_part, out_part)
    for k, pair, entries in ring(message, out_part // 2):
        crossed = across(pair) if shared else []
        size = pair[0].shape[0]
        for side, arrays in ((group, [(a, 0) for a in pair]), (1, crossed)):
            for i, ((array, base), entry) in enumerate(zip(arrays, entries)):
                offset = i * (out_part // 2) if k == half else 0
                out_plan.add(array, base, size, entry, 0, offset, side)

    other_states = lax.ppermute(prefix_states, "col", swap)
    other_actions = lax.ppermute(action_states, "col", swap)
    partial = prefix_partial(
        spot, at, prefix_states, other_states, prefix_gain, backbone_key, backbone_value
    )
    block = partial.shape[0] // count
    key_cols = backbone_key.shape[1]
    full = partial.shape[1]
    far = spot(at[0]).owner(half) * block
    sums = [
        lax.dynamic_slice(partial, (far, 0), (block, key_cols)),
        lax.dynamic_slice(partial, (far, key_cols), (block, full - key_cols)),
    ]
    for k in range(1, half + 1):
        got = around(sums)
        if k < half:
            sums = reduce_call(
                reduce_step_kernel,
                spot,
                at,
                partial,
                block,
                [2 * half - k, half - k],
                got,
                [full] * 2,
            )
        else:
            prefix_keys, prefix_values, keys_near, values_near = reduce_call(
                reduce_last_kernel, spot, at, partial, block, [0], got, [key_cols] * 4
            )

    states = (action_states, other_actions)
    key, value = project(spot, at, *states, kv_plan, [width, width])
    (query,) = project(spot, at, *states, query_plan, [query_cols], HEAD**-0.5 * LOG2E)

    groups = width // HEAD
    at_once = max(groups // 2, 1)
    attended = []
    for first in range(0, groups, at_once):
        attended.append(
            attend(
                prefix_length,
                action_length,
                query,
                key,
                value,
                keys_near,
                values_near,
                first,
                at_once,
            )
        )

    tokens = action_states.shape[0]

    def outward(side, dtype):
        return project_out(spot, at, attended, out_plan, out_rows, half, (), 0, tokens, side, dtype)

    given = lax.ppermute(outward(1, bf16), "col", swap)
    action_out = (outward(0, f32) + given.astype(f32)).astype(bf16)
    return (prefix_keys, prefix_values, action_out)


def shares(replicas, rows):
    return replicas == 2 and rows % 256 == 0


def solution(mesh):
    placed = (
        P(("groups", "col"), "row"),
        P("row"),
        P("row", "col"),
        P("row", "col"),
        P(("groups", "row"), "col"),
        P("row", "col"),
        P("row", "col"),
        P("row", "col"),
        P("col", "row"),
        P(("groups", "row")),
        P(("groups", "row")),
    )
    count, replicas = mesh.shape["row"], mesh.shape["groups"]

    def body(*args):
        return shards(count, replicas, *args)

    return jax.shard_map(
        body,
        mesh=mesh,
        in_specs=placed,
        out_specs=(
            P(("groups", "row"), "col"),
            P(("groups", "row"), "col"),
            P(("groups", "row"), "col"),
        ),
        check_vma=False,
    )
```

```python
import functools

import jax
import jax.numpy as jnp
from jax import lax
from jax.experimental import pallas as pl
from jax.experimental.pallas import tpu as pltpu
from jax.sharding import PartitionSpec as P


D = 8192
HEAD = 128
LOG2E = 1.4426950408889634


f32 = jnp.float32
bf16 = jnp.bfloat16
ANY = pl.BlockSpec(memory_space=pl.ANY)
NEAR = pl.BlockSpec(memory_space=pltpu.VMEM)


def ring_order(count):
    return list(range(0, count, 2)) + list(range(count - 1, 0, -2))


def ring_pairs(count, step):
    order = ring_order(count)
    return [(order[i], order[(i + step) % count]) for i in range(count)]


def spot_of(replicas):
    at = lax.axis_index("row") * 2 + lax.axis_index("col")
    return (at * replicas + lax.axis_index("groups")).astype(jnp.int32).reshape(1)


class Spot:
    def __init__(self, count, replicas, value):
        self.count = count
        self.group = lax.rem(value, replicas)
        self.col = lax.rem(lax.div(value, replicas), 2)
        self.row = lax.div(value, 2 * replicas)

    def owner(self, entry):
        count = self.count
        half = count // 2
        low = lax.div(self.row, 2)
        place = jnp.where(lax.rem(self.row, 2) == 0, low, count - 1 - low)
        place = lax.rem(place + (count - entry if entry <= half else entry - half), count)
        return jnp.where(place < half, 2 * place, 2 * (count - 1 - place) + 1)


def prefix_kernel(spot, at, mine, other, gain, key_w, value_w, out):
    per_half = pl.num_programs(0) // 2
    is_mine = pl.program_id(0) // per_half == spot(at[0]).col
    states = jnp.where(is_mine, mine[...], other[...]).astype(f32)
    squares = jnp.sum(states * states, axis=1, keepdims=True)
    scaled = (states * gain[...]).astype(bf16)
    cols = key_w.shape[1]
    out[:, :cols] = jnp.dot(scaled, key_w[...], preferred_element_type=f32).astype(bf16)
    out[:, cols : 2 * cols] = jnp.dot(scaled, value_w[...], preferred_element_type=f32).astype(bf16)
    out[:, 2 * cols :] = packed(squares)


def prefix_partial(spot, at, mine, other, gain, key_w, value_w):
    half_tokens, features = mine.shape
    tile = min(256, half_tokens)
    per_half = half_tokens // tile
    cols = key_w.shape[1]
    same = lambda i, p: (0, 0)
    return pl.pallas_call(
        functools.partial(prefix_kernel, spot),
        grid_spec=pltpu.PrefetchScalarGridSpec(
            num_scalar_prefetch=1,
            grid=(2 * per_half,),
            in_specs=[
                pl.BlockSpec((tile, features), lambda i, p: (i % per_half, 0)),
                pl.BlockSpec((tile, features), lambda i, p: (i % per_half, 0)),
                pl.BlockSpec((1, features), same),
                pl.BlockSpec((features, cols), same),
                pl.BlockSpec((features, cols), same),
            ],
            out_specs=pl.BlockSpec((tile, 2 * cols + HEAD), lambda i, p: (i, 0)),
        ),
        out_shape=jax.ShapeDtypeStruct((2 * half_tokens, 2 * cols + HEAD), bf16),
        compiler_params=pltpu.CompilerParams(vmem_limit_bytes=16 << 20),
        name="prefix_partial",
    )(at, mine, other, gain.reshape(1, -1), key_w, value_w)


def packed(squares):
    high = squares.astype(bf16)
    low = (squares - high.astype(f32)).astype(bf16)
    shape = (squares.shape[0], HEAD)
    lane = lax.broadcasted_iota(jnp.int32, shape, 1)
    return jnp.where(
        lane < HEAD // 2,
        jnp.broadcast_to(high.astype(f32), shape),
        jnp.broadcast_to(low.astype(f32), shape),
    ).astype(bf16)


def squares_of(tail):
    wide = tail.astype(f32)
    return wide[:, :1] + wide[:, HEAD // 2 : HEAD // 2 + 1]


def reduce_step_kernel(at, block_up, block_down, got_up, got_down, up, down):
    full = up.shape[1] - HEAD
    for block, got, out in ((block_up, got_up, up), (block_down, got_down, down)):
        width = got.shape[1]
        if width == full // 2:
            low, high = 0, width
        elif width == full // 2 + HEAD:
            low, high = full // 2, full
        else:
            low, high = 0, full
        if low > 0:
            out[:, :low] = block[:, :low]
        total = block[:, low:high].astype(f32) + got[:, : high - low].astype(f32)
        out[:, low:high] = total.astype(bf16)
        if high < full:
            out[:, high:] = block[:, high:]
        else:
            out[:, full:] = packed(squares_of(block[:, full:]) + squares_of(got[:, high - low :]))


def reduce_last_kernel(at, block, got_up, got_down, keys, values, keys_too, values_too):
    cols = keys.shape[1]
    total = block[:, : 2 * cols].astype(f32) + got_up[:, : 2 * cols].astype(f32)
    total = total + got_down[:, : 2 * cols].astype(f32)
    squares = squares_of(block[:, 2 * cols :])
    squares = squares + squares_of(got_up[:, 2 * cols :]) + squares_of(got_down[:, 2 * cols :])
    total = total * lax.rsqrt(squares / D + 1e-06)
    for out in (keys, keys_too):
        out[...] = total[:, :cols].astype(bf16)
    for out in (values, values_too):
        out[...] = total[:, cols:].astype(bf16)


def reduce_call(kernel, spot, at, partial, block, places, got, widths):
    whole = lambda a: pl.BlockSpec(a, lambda i, t: (0, 0))
    taken = [
        pl.BlockSpec((block, partial.shape[1]), functools.partial(lambda n, i, t: (spot(t[0]).owner(n), 0), n))
        for n in places
    ]
    return pl.pallas_call(
        kernel,
        grid_spec=pltpu.PrefetchScalarGridSpec(
            num_scalar_prefetch=1,
            grid=(1,),
            in_specs=taken + [whole(g.shape) for g in got],
            out_specs=[whole((block, w)) for w in widths],
        ),
        out_shape=[jax.ShapeDtypeStruct((block, w), bf16) for w in widths],
        compiler_params=pltpu.CompilerParams(vmem_limit_bytes=8 << 20),
    )(at, *[partial] * len(places), *got)


class Plan:
    def __init__(self, rows, width, segments):
        self.rows, self.width, self.segments = rows, width, segments
        self.copies, self.refs = [], []

    def add(self, array, low, count, entry, segment, offset=0, group=None):
        for at, known in enumerate(self.refs):
            if known is array:
                break
        else:
            at = len(self.refs)
            self.refs.append(array)
        self.copies.append((at, low, count, entry, segment, offset, group))


def project_kernel(plan, scale, spot, at, mine, other, *refs):
    sources = refs[: len(plan.refs)]
    *outs, weights, sems = refs[len(plan.refs) :]
    rows, width = plan.rows, plan.width
    half_features = mine.shape[1]
    features = 2 * half_features
    here = spot(at[0])

    def copies(segment):
        for index, (ref, low, count, entry, to, offset, group) in enumerate(plan.copies):
            if to != segment:
                continue
            row = here.owner(entry) * rows + features - here.col * half_features
            row = lax.rem(row, features)
            row = row + offset
            if group is not None:
                row = row + (here.group if group == 0 else 1 - here.group) * count
            source = sources[ref]
            col = to * width if source.shape[1] > width else 0
            yield pltpu.make_async_copy(
                source.at[low : low + count, col : col + width],
                weights.at[
                    pl.ds(pl.multiple_of(row, count), count), to * width : (to + 1) * width
                ],
                sems.at[index],
            )

    for segment in range(plan.segments):
        for copy in copies(segment):
            copy.start()
    for segment in range(plan.segments):
        for copy in copies(segment):
            copy.wait()
        cols = slice(segment * width, (segment + 1) * width)
        total = jnp.dot(mine[...], weights[:half_features, cols], preferred_element_type=f32)
        total += jnp.dot(other[...], weights[half_features:, cols], preferred_element_type=f32)
        if scale is not None:
            total = total * scale
        if len(outs) == plan.segments:
            outs[segment][...] = total.astype(bf16)
        else:
            outs[0][:, cols] = total.astype(bf16)


def project(spot, at, mine, other, plan, widths, scale=None):
    tokens, half_features = mine.shape
    return pl.pallas_call(
        functools.partial(project_kernel, plan, scale, spot),
        grid_spec=pltpu.PrefetchScalarGridSpec(
            num_scalar_prefetch=1,
            grid=(1,),
            in_specs=[NEAR] * 2 + [ANY] * len(plan.refs),
            out_specs=[NEAR] * len(widths),
            scratch_shapes=[
                pltpu.VMEM((2 * half_features, plan.segments * plan.width), bf16),
                pltpu.SemaphoreType.DMA((len(plan.copies),)),
            ],
        ),
        out_shape=[pltpu.VMEM((tokens, w), bf16) for w in widths],
        compiler_params=pltpu.CompilerParams(vmem_limit_bytes=24 << 20),
        name="project",
    )(at, mine, other, *plan.refs)


def attend_kernel(prefix_length, action_length, query, key, value, prefix_key, prefix_value, out, keys, values):
    prefix_count = prefix_key.shape[0]
    count = key.shape[0]
    total = prefix_count + count
    tile = min(256, query.shape[0])

    keys[:count, :HEAD] = key[...]
    keys[count:, :HEAD] = prefix_key[...]
    at = lax.broadcasted_iota(jnp.int32, (total, HEAD), 0)
    lane = lax.broadcasted_iota(jnp.int32, (total, HEAD), 1)
    limit = jnp.where(at < count, action_length[0], prefix_length[0] + count)
    keys[:, HEAD:] = jnp.where((at >= limit) & (lane == 0), -1e30, 0.0).astype(bf16)
    values[:count, :HEAD] = value[...]
    values[count:, :HEAD] = prefix_value[...]
    values[:, HEAD:] = jnp.ones((total, HEAD), bf16)
    ones = jnp.ones((tile, HEAD), bf16)

    def place(unit):
        head, at = unit
        return slice(at * tile, (at + 1) * tile), slice(head * HEAD, (head + 1) * HEAD)

    def score(unit):
        wide = jnp.concatenate([query[place(unit)], ones], axis=1)
        return lax.dot_general(
            wide, keys[...], (((1,), (1,)), ((), ())), preferred_element_type=f32
        )

    units = [(head, at) for at in range(query.shape[0] // tile) for head in range(2)]
    following = score(units[0])
    for index, unit in enumerate(units):
        scores = following
        if index + 1 < len(units):
            following = score(units[index + 1])
        highest = jnp.max(scores, axis=1, keepdims=True)
        weights = jnp.exp2(scores - highest).astype(bf16)
        both = jnp.dot(weights, values[...], preferred_element_type=f32)
        out[place(unit)] = (both[:, :HEAD] / both[:, HEAD:]).astype(bf16)


def attend(prefix_length, action_length, query, key, value, prefix_key, prefix_value, first, groups):
    tokens = query.shape[0]
    prefix_count = prefix_key.shape[0]
    total = tokens + prefix_count
    at = lambda g, *_: (0, first + g)
    return pl.pallas_call(
        attend_kernel,
        grid_spec=pltpu.PrefetchScalarGridSpec(
            num_scalar_prefetch=2,
            grid=(groups,),
            in_specs=[
                pl.BlockSpec((tokens, 2 * HEAD), at),
                pl.BlockSpec((tokens, HEAD), at),
                pl.BlockSpec((tokens, HEAD), at),
                pl.BlockSpec((prefix_count, HEAD), at),
                pl.BlockSpec((prefix_count, HEAD), at),
            ],
            out_specs=pl.BlockSpec((tokens, 2 * HEAD), lambda g, *_: (0, g)),
            scratch_shapes=[
                pltpu.VMEM((total, 2 * HEAD), bf16),
                pltpu.VMEM((total, 2 * HEAD), bf16),
            ],
        ),
        out_shape=jax.ShapeDtypeStruct((tokens, groups * 2 * HEAD), bf16),
        compiler_params=pltpu.CompilerParams(vmem_limit_bytes=16 << 20),
        name="attend",
    )(prefix_length, action_length, query, key, value, prefix_key, prefix_value)


def out_kernel(plan, side, parts, spot, at, *refs):
    place = spot(at[0])
    attended = refs[:parts]
    sources = refs[parts : parts + len(plan.refs)]
    got = refs[parts + len(plan.refs) : -3]
    out, weights, sems = refs[-3:]
    rows, cols = weights.shape[0], plan.width
    half = weights.shape[1] // cols
    quarter = rows // 4
    first = pl.program_id(0) == 0

    @pl.when(first)
    def _():
        for ref, low, count, entry, _, offset, group in plan.copies:
            owner = place.owner(entry)
            to = lax.rem(owner, half)
            mine = owner // half == place.col
            here = mine if side == 0 else jnp.logical_not(mine)
            first_quarter = offset // quarter
            if group is not None:
                first_quarter += 2 * (place.group if group == 0 else 1 - place.group)

            @pl.when(here)
            def _():
                for i in range(count // quarter):
                    row = pl.multiple_of((first_quarter + i) * quarter, quarter)
                    pltpu.make_async_copy(
                        sources[ref].at[low + i * quarter : low + (i + 1) * quarter],
                        weights.at[
                            pl.ds(row, quarter), pl.ds(pl.multiple_of(to * cols, cols), cols)
                        ],
                        sems.at[first_quarter + i, to],
                    ).start()

        for to in range(half):
            for i in range(4):
                pltpu.make_async_copy(
                    sources[0].at[:quarter],
                    weights.at[i * quarter : (i + 1) * quarter, to * cols : (to + 1) * cols],
                    sems.at[i, to],
                ).wait()

    depth = rows // parts
    tile = out.shape[0]
    here = pl.ds(pl.multiple_of(pl.program_id(0) * tile, tile), tile)
    total = jnp.dot(attended[0][here], weights[:depth], preferred_element_type=f32)
    for j in range(1, parts):
        total += jnp.dot(
            attended[j][here], weights[j * depth : (j + 1) * depth], preferred_element_type=f32
        )
    if len(got) == 1:
        total += got[0][...].astype(f32)
    elif len(got) == 2:
        early = pl.program_id(0) < pl.num_programs(0) - 1
        total += jnp.where(early, got[0][...], got[1][...]).astype(f32)
    out[...] = total.astype(out.dtype)


def project_out(spot, at, attended, plan, rows, half, got, size, side, dtype):
    tile = min(512, size)
    width = half * plan.width
    parts = len(attended)
    args = [at, *attended, *plan.refs, *got]
    specs = [NEAR] * parts
    specs += [ANY] * len(plan.refs)
    for array in got:
        last = array.shape[0] // tile - 1
        specs.append(
            pl.BlockSpec(
                (tile, width), functools.partial(lambda n, i, *_: (jnp.minimum(i, n), 0), last)
            )
        )
    return pl.pallas_call(
        functools.partial(out_kernel, plan, side, parts, spot),
        grid_spec=pltpu.PrefetchScalarGridSpec(
            num_scalar_prefetch=1,
            grid=(size // tile,),
            in_specs=specs,
            out_specs=pl.BlockSpec((tile, width), lambda i, *_: (i, 0)),
            scratch_shapes=[
                pltpu.VMEM((rows, width), bf16),
                pltpu.SemaphoreType.DMA((4, half)),
            ],
        ),
        out_shape=pltpu.VMEM((size, width), f32)
        if side == 0
        else jax.ShapeDtypeStruct((size, width), dtype),
        compiler_params=pltpu.CompilerParams(vmem_limit_bytes=24 << 20),
        name="project_out",
    )(*args)


def add_kernel(kept, given, out):
    tile = out.shape[0]
    here = pl.ds(pl.multiple_of(pl.program_id(0) * tile, tile), tile)
    out[...] = (kept[here] + given[here].astype(f32)).astype(bf16)


def add(kept, given):
    tokens, width = kept.shape
    tile = min(256, tokens)
    return pl.pallas_call(
        add_kernel,
        grid=(tokens // tile,),
        in_specs=[NEAR] * 2,
        out_specs=pl.BlockSpec((tile, width), lambda i: (i, 0)),
        out_shape=jax.ShapeDtypeStruct((tokens, width), bf16),
        compiler_params=pltpu.CompilerParams(vmem_limit_bytes=16 << 20),
        name="add",
    )(kept, given)


def shards(
    count,
    replicas,
    prefix_states,
    prefix_gain,
    backbone_key,
    backbone_value,
    action_states,
    expert_query,
    expert_key,
    expert_value,
    expert_out,
    prefix_length,
    action_length,
):
    half = count // 2
    up, down = ring_pairs(count, 1), ring_pairs(count, -1)
    swap = [(0, 1), (1, 0)]
    spot = functools.partial(Spot, count, replicas)
    at = spot_of(replicas)
    rows, width = expert_key.shape
    query_cols = expert_query.shape[1]
    out_rows, out_cols = expert_out.shape

    shared = shares(replicas, rows)
    part = rows // 2 if shared else rows
    group = 0 if shared else None

    def own_half(array, low, width):
        if shared:
            return lax.dynamic_slice(array, (lax.axis_index("groups") * part, low), (part, width))
        return array[:, low : low + width]

    def around(pair):
        return [lax.ppermute(pair[0], "row", up), lax.ppermute(pair[1], "row", down)]

    def across(pair):
        joined = jnp.concatenate(pair, axis=0) if len(pair) > 1 else pair[0]
        joined = lax.ppermute(joined, "groups", swap)
        return [(joined, i * a.shape[0]) for i, a in enumerate(pair)]

    def ring(block, cut):
        pair = [block, block]
        for k in range(1, half + 1):
            if k == half:
                pair = [pair[0][:cut], pair[1][cut:]]
            pair = around(pair)
            yield k, pair, (k, half + k if k < half else half)

    strips = query_cols // width
    kv_plan, query_plan = Plan(rows, width, 2), Plan(rows, width, strips)
    kv_plan.add(expert_key, 0, rows, 0, 0)
    kv_plan.add(expert_value, 0, rows, 0, 1)
    for segment in range(strips):
        query_plan.add(expert_query, 0, rows, 0, segment)
    cut = (strips - 1) * part
    pair = jnp.concatenate([own_half(expert_key, 0, width), own_half(expert_value, 0, width)], axis=0)
    pair = [pair, pair]
    rest = [own_half(expert_query, i * width, width) for i in range(strips - 1)]
    rest = jnp.concatenate([*rest, expert_query[:, (strips - 1) * width :]], axis=0)
    rest = [rest, rest]
    for k in range(1, half + 1):
        entries = [k, half + k] if k < half else [half, half]
        if k == half:
            pair, rest = [pair[0][:part], pair[1][part:]], [rest[0][:cut], rest[1][cut:]]
        pair, rest = around(pair), around(rest)
        crossed = across(pair) if shared else []
        for side, arrays in ((group, [(a, 0) for a in pair]), (1, crossed)):
            for i, ((array, base), entry) in enumerate(zip(arrays, entries)):
                for segment in range(2) if k < half else [i]:
                    low = base + (segment * part if k < half else 0)
                    kv_plan.add(array, low, part, entry, segment, 0, side)
        split = [r[:cut] for r in rest] if k < half else rest[:1]
        crossed = across(split) if shared else []
        arrays = [(a, 0) for a in (rest if k < half else rest[:1])]
        for side, arrays in ((group, arrays), (1, crossed)):
            for (array, base), entry in zip(arrays, entries):
                for segment in range(strips - 1):
                    query_plan.add(array, base + segment * part, part, entry, segment, 0, side)
        for array, entry in zip(rest if k < half else rest[1:], entries):
            query_plan.add(array, cut if k < half else 0, rows, entry, strips - 1)

    out_plan = Plan(out_rows, out_cols, 1)
    out_plan.add(expert_out, 0, out_rows, 0, 0)
    out_part = out_rows // 2 if shared else out_rows
    message = expert_out
    if shared:
        message = lax.dynamic_slice_in_dim(expert_out, lax.axis_index("groups") * out_part, out_part)
    for k, pair, entries in ring(message, out_part // 2):
        crossed = across(pair) if shared else []
        size = pair[0].shape[0]
        for side, arrays in ((group, [(a, 0) for a in pair]), (1, crossed)):
            for i, ((array, base), entry) in enumerate(zip(arrays, entries)):
                offset = i * (out_part // 2) if k == half else 0
                out_plan.add(array, base, size, entry, 0, offset, side)

    other_states = lax.ppermute(prefix_states, "col", swap)
    other_actions = lax.ppermute(action_states, "col", swap)
    partial = prefix_partial(
        spot, at, prefix_states, other_states, prefix_gain, backbone_key, backbone_value
    )
    block = partial.shape[0] // count
    key_cols = backbone_key.shape[1]
    full = partial.shape[1]
    far = spot(at[0]).owner(half) * block
    sums = [
        lax.dynamic_slice(partial, (far, 0), (block, key_cols)),
        lax.dynamic_slice(partial, (far, key_cols), (block, full - key_cols)),
    ]
    for k in range(1, half + 1):
        got = around(sums)
        if k < half:
            sums = reduce_call(
                reduce_step_kernel,
                spot,
                at,
                partial,
                block,
                [2 * half - k, half - k],
                got,
                [full] * 2,
            )
        else:
            prefix_keys, prefix_values, keys_near, values_near = reduce_call(
                reduce_last_kernel, spot, at, partial, block, [0], got, [key_cols] * 4
            )

    states = (action_states, other_actions)
    key, value = project(spot, at, *states, kv_plan, [width, width])
    (query,) = project(spot, at, *states, query_plan, [query_cols], HEAD**-0.5 * LOG2E)

    groups = width // HEAD
    at_once = max(groups // 2, 1)
    attended = []
    for first in range(0, groups, at_once):
        attended.append(
            attend(
                prefix_length,
                action_length,
                query,
                key,
                value,
                keys_near,
                values_near,
                first,
                at_once,
            )
        )

    tokens = action_states.shape[0]

    def outward(side, dtype):
        return project_out(spot, at, attended, out_plan, out_rows, half, (), tokens, side, dtype)

    given = lax.ppermute(outward(1, bf16), "col", swap)
    action_out = add(outward(0, f32), given)
    return (prefix_keys, prefix_values, action_out)


def shares(replicas, rows):
    return replicas == 2 and rows % 256 == 0


def solution(mesh):
    placed = (
        P(("groups", "col"), "row"),
        P("row"),
        P("row", "col"),
        P("row", "col"),
        P(("groups", "row"), "col"),
        P("row", "col"),
        P("row", "col"),
        P("row", "col"),
        P("col", "row"),
        P(("groups", "row")),
        P(("groups", "row")),
    )
    count, replicas = mesh.shape["row"], mesh.shape["groups"]

    def body(*args):
        return shards(count, replicas, *args)

    return jax.shard_map(
        body,
        mesh=mesh,
        in_specs=placed,
        out_specs=(
            P(("groups", "row"), "col"),
            P(("groups", "row"), "col"),
            P(("groups", "row"), "col"),
        ),
        check_vma=False,
    )
```

```python
import functools

import jax
import jax.numpy as jnp
from jax import lax
from jax.experimental import pallas as pl
from jax.experimental.pallas import tpu as pltpu
from jax.sharding import PartitionSpec as P


D = 8192
HEAD = 128
LOG2E = 1.4426950408889634


f32 = jnp.float32
bf16 = jnp.bfloat16
ANY = pl.BlockSpec(memory_space=pl.ANY)
NEAR = pl.BlockSpec(memory_space=pltpu.VMEM)


def ring_order(count):
    return list(range(0, count, 2)) + list(range(count - 1, 0, -2))


def ring_pairs(count, step):
    order = ring_order(count)
    return [(order[i], order[(i + step) % count]) for i in range(count)]


def spot_of(replicas):
    at = lax.axis_index("row") * 2 + lax.axis_index("col")
    return (at * replicas + lax.axis_index("groups")).astype(jnp.int32).reshape(1)


class Spot:
    def __init__(self, count, replicas, value):
        self.count = count
        self.group = lax.rem(value, replicas)
        self.col = lax.rem(lax.div(value, replicas), 2)
        self.row = lax.div(value, 2 * replicas)

    def owner(self, entry):
        count = self.count
        half = count // 2
        low = lax.div(self.row, 2)
        place = jnp.where(lax.rem(self.row, 2) == 0, low, count - 1 - low)
        place = lax.rem(place + (count - entry if entry <= half else entry - half), count)
        return jnp.where(place < half, 2 * place, 2 * (count - 1 - place) + 1)


def prefix_kernel(spot, at, mine, other, gain, key_w, value_w, out):
    per_half = pl.num_programs(0) // 2
    is_mine = pl.program_id(0) // per_half == spot(at[0]).col
    states = jnp.where(is_mine, mine[...], other[...]).astype(f32)
    squares = jnp.sum(states * states, axis=1, keepdims=True)
    scaled = (states * gain[...]).astype(bf16)
    cols = key_w.shape[1]
    out[:, :cols] = jnp.dot(scaled, key_w[...], preferred_element_type=f32).astype(bf16)
    out[:, cols : 2 * cols] = jnp.dot(scaled, value_w[...], preferred_element_type=f32).astype(bf16)
    out[:, 2 * cols :] = packed(squares)


def prefix_partial(spot, at, mine, other, gain, key_w, value_w):
    half_tokens, features = mine.shape
    tile = min(256, half_tokens)
    per_half = half_tokens // tile
    cols = key_w.shape[1]
    same = lambda i, p: (0, 0)
    return pl.pallas_call(
        functools.partial(prefix_kernel, spot),
        grid_spec=pltpu.PrefetchScalarGridSpec(
            num_scalar_prefetch=1,
            grid=(2 * per_half,),
            in_specs=[
                pl.BlockSpec((tile, features), lambda i, p: (i % per_half, 0)),
                pl.BlockSpec((tile, features), lambda i, p: (i % per_half, 0)),
                pl.BlockSpec((1, features), same),
                pl.BlockSpec((features, cols), same),
                pl.BlockSpec((features, cols), same),
            ],
            out_specs=pl.BlockSpec((tile, 2 * cols + HEAD), lambda i, p: (i, 0)),
        ),
        out_shape=jax.ShapeDtypeStruct((2 * half_tokens, 2 * cols + HEAD), bf16),
        compiler_params=pltpu.CompilerParams(vmem_limit_bytes=16 << 20),
        name="prefix_partial",
    )(at, mine, other, gain.reshape(1, -1), key_w, value_w)


def packed(squares):
    high = squares.astype(bf16)
    low = (squares - high.astype(f32)).astype(bf16)
    shape = (squares.shape[0], HEAD)
    lane = lax.broadcasted_iota(jnp.int32, shape, 1)
    return jnp.where(
        lane < HEAD // 2,
        jnp.broadcast_to(high.astype(f32), shape),
        jnp.broadcast_to(low.astype(f32), shape),
    ).astype(bf16)


def squares_of(tail):
    wide = tail.astype(f32)
    return wide[:, :1] + wide[:, HEAD // 2 : HEAD // 2 + 1]


def reduce_step_kernel(at, block_up, block_down, got_up, got_down, up, down):
    full = up.shape[1] - HEAD
    for block, got, out in ((block_up, got_up, up), (block_down, got_down, down)):
        width = got.shape[1]
        if width == full // 2:
            low, high = 0, width
        elif width == full // 2 + HEAD:
            low, high = full // 2, full
        else:
            low, high = 0, full
        if low > 0:
            out[:, :low] = block[:, :low]
        total = block[:, low:high].astype(f32) + got[:, : high - low].astype(f32)
        out[:, low:high] = total.astype(bf16)
        if high < full:
            out[:, high:] = block[:, high:]
        else:
            out[:, full:] = packed(squares_of(block[:, full:]) + squares_of(got[:, high - low :]))


def reduce_last_kernel(at, block, got_up, got_down, keys, values, keys_too, values_too):
    cols = keys.shape[1]
    total = block[:, : 2 * cols].astype(f32) + got_up[:, : 2 * cols].astype(f32)
    total = total + got_down[:, : 2 * cols].astype(f32)
    squares = squares_of(block[:, 2 * cols :])
    squares = squares + squares_of(got_up[:, 2 * cols :]) + squares_of(got_down[:, 2 * cols :])
    total = total * lax.rsqrt(squares / D + 1e-06)
    for out in (keys, keys_too):
        out[...] = total[:, :cols].astype(bf16)
    for out in (values, values_too):
        out[...] = total[:, cols:].astype(bf16)


def reduce_call(kernel, spot, at, partial, block, places, got, widths):
    whole = lambda a: pl.BlockSpec(a, lambda i, t: (0, 0))
    taken = [
        pl.BlockSpec((block, partial.shape[1]), functools.partial(lambda n, i, t: (spot(t[0]).owner(n), 0), n))
        for n in places
    ]
    return pl.pallas_call(
        kernel,
        grid_spec=pltpu.PrefetchScalarGridSpec(
            num_scalar_prefetch=1,
            grid=(1,),
            in_specs=taken + [whole(g.shape) for g in got],
            out_specs=[whole((block, w)) for w in widths],
        ),
        out_shape=[jax.ShapeDtypeStruct((block, w), bf16) for w in widths],
        compiler_params=pltpu.CompilerParams(vmem_limit_bytes=8 << 20),
    )(at, *[partial] * len(places), *got)


class Plan:
    def __init__(self, rows, width, segments):
        self.rows, self.width, self.segments = rows, width, segments
        self.copies, self.refs = [], []

    def add(self, array, low, count, entry, segment, offset=0, group=None):
        for at, known in enumerate(self.refs):
            if known is array:
                break
        else:
            at = len(self.refs)
            self.refs.append(array)
        self.copies.append((at, low, count, entry, segment, offset, group))


def project_kernel(plan, scale, spot, at, mine, other, *refs):
    sources = refs[: len(plan.refs)]
    *outs, weights, sems = refs[len(plan.refs) :]
    rows, width = plan.rows, plan.width
    half_features = mine.shape[1]
    features = 2 * half_features
    here = spot(at[0])

    def copies(segment):
        for index, (ref, low, count, entry, to, offset, group) in enumerate(plan.copies):
            if to != segment:
                continue
            row = here.owner(entry) * rows + features - here.col * half_features
            row = lax.rem(row, features)
            row = row + offset
            if group is not None:
                row = row + (here.group if group == 0 else 1 - here.group) * count
            source = sources[ref]
            col = to * width if source.shape[1] > width else 0
            yield pltpu.make_async_copy(
                source.at[low : low + count, col : col + width],
                weights.at[
                    pl.ds(pl.multiple_of(row, count), count), to * width : (to + 1) * width
                ],
                sems.at[index],
            )

    for segment in range(plan.segments):
        for copy in copies(segment):
            copy.start()
    for segment in range(plan.segments):
        for copy in copies(segment):
            copy.wait()
        cols = slice(segment * width, (segment + 1) * width)
        total = jnp.dot(mine[...], weights[:half_features, cols], preferred_element_type=f32)
        total += jnp.dot(other[...], weights[half_features:, cols], preferred_element_type=f32)
        if scale is not None:
            total = total * scale
        if len(outs) == plan.segments:
            outs[segment][...] = total.astype(bf16)
        else:
            outs[0][:, cols] = total.astype(bf16)


def project(spot, at, mine, other, plan, widths, scale=None):
    tokens, half_features = mine.shape
    return pl.pallas_call(
        functools.partial(project_kernel, plan, scale, spot),
        grid_spec=pltpu.PrefetchScalarGridSpec(
            num_scalar_prefetch=1,
            grid=(1,),
            in_specs=[NEAR] * 2 + [ANY] * len(plan.refs),
            out_specs=[NEAR] * len(widths),
            scratch_shapes=[
                pltpu.VMEM((2 * half_features, plan.segments * plan.width), bf16),
                pltpu.SemaphoreType.DMA((len(plan.copies),)),
            ],
        ),
        out_shape=[pltpu.VMEM((tokens, w), bf16) for w in widths],
        compiler_params=pltpu.CompilerParams(vmem_limit_bytes=24 << 20),
        name="project",
    )(at, mine, other, *plan.refs)


def attend_kernel(prefix_length, action_length, query, key, value, prefix_key, prefix_value, out, keys, values):
    prefix_count = prefix_key.shape[0]
    count = key.shape[0]
    total = prefix_count + count
    tile = min(256, query.shape[0])

    keys[:count, :HEAD] = key[...]
    keys[count:, :HEAD] = prefix_key[...]
    at = lax.broadcasted_iota(jnp.int32, (total, HEAD), 0)
    lane = lax.broadcasted_iota(jnp.int32, (total, HEAD), 1)
    limit = jnp.where(at < count, action_length[0], prefix_length[0] + count)
    keys[:, HEAD:] = jnp.where((at >= limit) & (lane == 0), -1e30, 0.0).astype(bf16)
    values[:count, :HEAD] = value[...]
    values[count:, :HEAD] = prefix_value[...]
    values[:, HEAD:] = jnp.ones((total, HEAD), bf16)
    ones = jnp.ones((tile, HEAD), bf16)

    def place(unit):
        head, at = unit
        return slice(at * tile, (at + 1) * tile), slice(head * HEAD, (head + 1) * HEAD)

    def score(unit):
        wide = jnp.concatenate([query[place(unit)], ones], axis=1)
        return lax.dot_general(
            wide, keys[...], (((1,), (1,)), ((), ())), preferred_element_type=f32
        )

    units = [(head, at) for at in range(query.shape[0] // tile) for head in range(2)]
    following = score(units[0])
    for index, unit in enumerate(units):
        scores = following
        if index + 1 < len(units):
            following = score(units[index + 1])
        highest = jnp.max(scores, axis=1, keepdims=True)
        weights = jnp.exp2(scores - highest).astype(bf16)
        both = jnp.dot(weights, values[...], preferred_element_type=f32)
        out[place(unit)] = (both[:, :HEAD] / both[:, HEAD:]).astype(bf16)


def attend(prefix_length, action_length, query, key, value, prefix_key, prefix_value, first, groups):
    tokens = query.shape[0]
    prefix_count = prefix_key.shape[0]
    total = tokens + prefix_count
    at = lambda g, *_: (0, first + g)
    return pl.pallas_call(
        attend_kernel,
        grid_spec=pltpu.PrefetchScalarGridSpec(
            num_scalar_prefetch=2,
            grid=(groups,),
            in_specs=[
                pl.BlockSpec((tokens, 2 * HEAD), at),
                pl.BlockSpec((tokens, HEAD), at),
                pl.BlockSpec((tokens, HEAD), at),
                pl.BlockSpec((prefix_count, HEAD), at),
                pl.BlockSpec((prefix_count, HEAD), at),
            ],
            out_specs=pl.BlockSpec((tokens, 2 * HEAD), lambda g, *_: (0, g)),
            scratch_shapes=[
                pltpu.VMEM((total, 2 * HEAD), bf16),
                pltpu.VMEM((total, 2 * HEAD), bf16),
            ],
        ),
        out_shape=jax.ShapeDtypeStruct((tokens, groups * 2 * HEAD), bf16),
        compiler_params=pltpu.CompilerParams(vmem_limit_bytes=16 << 20),
        name="attend",
    )(prefix_length, action_length, query, key, value, prefix_key, prefix_value)


def out_kernel(plan, side, parts, spot, at, *refs):
    place = spot(at[0])
    attended = refs[:parts]
    sources = refs[parts : parts + len(plan.refs)]
    got = refs[parts + len(plan.refs) : -3]
    out, weights, sems = refs[-3:]
    rows, cols = weights.shape[0], plan.width
    half = weights.shape[1] // cols
    quarter = rows // 4
    first = pl.program_id(0) == 0

    @pl.when(first)
    def _():
        for ref, low, count, entry, _, offset, group in plan.copies:
            owner = place.owner(entry)
            to = lax.rem(owner, half)
            mine = owner // half == place.col
            here = mine if side == 0 else jnp.logical_not(mine)
            first_quarter = offset // quarter
            if group is not None:
                first_quarter += 2 * (place.group if group == 0 else 1 - place.group)

            @pl.when(here)
            def _():
                for i in range(count // quarter):
                    row = pl.multiple_of((first_quarter + i) * quarter, quarter)
                    pltpu.make_async_copy(
                        sources[ref].at[low + i * quarter : low + (i + 1) * quarter],
                        weights.at[
                            pl.ds(row, quarter), pl.ds(pl.multiple_of(to * cols, cols), cols)
                        ],
                        sems.at[first_quarter + i, to],
                    ).start()

        for to in range(half):
            for i in range(4):
                pltpu.make_async_copy(
                    sources[0].at[:quarter],
                    weights.at[i * quarter : (i + 1) * quarter, to * cols : (to + 1) * cols],
                    sems.at[i, to],
                ).wait()

    depth = rows // parts
    tile = out.shape[0]
    here = pl.ds(pl.multiple_of(pl.program_id(0) * tile, tile), tile)
    total = jnp.dot(attended[0][here], weights[:depth], preferred_element_type=f32)
    for j in range(1, parts):
        total += jnp.dot(
            attended[j][here], weights[j * depth : (j + 1) * depth], preferred_element_type=f32
        )
    if len(got) == 1:
        total += got[0][...].astype(f32)
    elif len(got) == 2:
        early = pl.program_id(0) < pl.num_programs(0) - 1
        total += jnp.where(early, got[0][...], got[1][...]).astype(f32)
    out[...] = total.astype(out.dtype)


def project_out(spot, at, attended, plan, rows, half, got, size, side, dtype):
    tile = min(512, size)
    width = half * plan.width
    parts = len(attended)
    args = [at, *attended, *plan.refs, *got]
    specs = [NEAR] * parts
    specs += [ANY] * len(plan.refs)
    for array in got:
        last = array.shape[0] // tile - 1
        specs.append(
            pl.BlockSpec(
                (tile, width), functools.partial(lambda n, i, *_: (jnp.minimum(i, n), 0), last)
            )
        )
    return pl.pallas_call(
        functools.partial(out_kernel, plan, side, parts, spot),
        grid_spec=pltpu.PrefetchScalarGridSpec(
            num_scalar_prefetch=1,
            grid=(size // tile,),
            in_specs=specs,
            out_specs=pl.BlockSpec((tile, width), lambda i, *_: (i, 0)),
            scratch_shapes=[
                pltpu.VMEM((rows, width), bf16),
                pltpu.SemaphoreType.DMA((4, half)),
            ],
        ),
        out_shape=pltpu.VMEM((size, width), f32)
        if side == 0
        else jax.ShapeDtypeStruct((size, width), dtype),
        compiler_params=pltpu.CompilerParams(vmem_limit_bytes=24 << 20),
        name="project_out",
    )(*args)


def join_kernel(first, second, out):
    rows = first.shape[0]
    out[:rows] = first[...]
    out[rows:] = second[...]


def join(pair, rows):
    width = pair[0].shape[1]
    return pl.pallas_call(
        join_kernel,
        grid=(1,),
        in_specs=[pl.BlockSpec((rows, width), lambda i: (0, 0))] * 2,
        out_specs=pl.BlockSpec((2 * rows, width), lambda i: (0, 0)),
        out_shape=jax.ShapeDtypeStruct((2 * rows, width), bf16),
        compiler_params=pltpu.CompilerParams(vmem_limit_bytes=8 << 20),
        name="join",
    )(*pair)


def add_kernel(kept, given, out):
    tile = out.shape[0]
    here = pl.ds(pl.multiple_of(pl.program_id(0) * tile, tile), tile)
    out[...] = (kept[here] + given[here].astype(f32)).astype(bf16)


def add(kept, given):
    tokens, width = kept.shape
    tile = min(256, tokens)
    return pl.pallas_call(
        add_kernel,
        grid=(tokens // tile,),
        in_specs=[NEAR] * 2,
        out_specs=pl.BlockSpec((tile, width), lambda i: (i, 0)),
        out_shape=jax.ShapeDtypeStruct((tokens, width), bf16),
        compiler_params=pltpu.CompilerParams(vmem_limit_bytes=16 << 20),
        name="add",
    )(kept, given)


def shards(
    count,
    replicas,
    prefix_states,
    prefix_gain,
    backbone_key,
    backbone_value,
    action_states,
    expert_query,
    expert_key,
    expert_value,
    expert_out,
    prefix_length,
    action_length,
):
    half = count // 2
    up, down = ring_pairs(count, 1), ring_pairs(count, -1)
    swap = [(0, 1), (1, 0)]
    spot = functools.partial(Spot, count, replicas)
    at = spot_of(replicas)
    rows, width = expert_key.shape
    query_cols = expert_query.shape[1]
    out_rows, out_cols = expert_out.shape

    shared = shares(replicas, rows)
    part = rows // 2 if shared else rows
    group = 0 if shared else None

    def own_half(array, low, width):
        if shared:
            return lax.dynamic_slice(array, (lax.axis_index("groups") * part, low), (part, width))
        return array[:, low : low + width]

    def around(pair):
        return [lax.ppermute(pair[0], "row", up), lax.ppermute(pair[1], "row", down)]

    def across(pair, size=None):
        size = size or pair[0].shape[0]
        joined = join(pair, size) if len(pair) > 1 else pair[0]
        joined = lax.ppermute(joined, "groups", swap)
        return [(joined, i * size) for i in range(len(pair))]

    def ring(block, cut):
        pair = [block, block]
        for k in range(1, half + 1):
            if k == half:
                pair = [pair[0][:cut], pair[1][cut:]]
            pair = around(pair)
            yield k, pair, (k, half + k if k < half else half)

    strips = query_cols // width
    kv_plan, query_plan = Plan(rows, width, 2), Plan(rows, width, strips)
    kv_plan.add(expert_key, 0, rows, 0, 0)
    kv_plan.add(expert_value, 0, rows, 0, 1)
    for segment in range(strips):
        query_plan.add(expert_query, 0, rows, 0, segment)
    cut = (strips - 1) * part
    pair = jnp.concatenate([own_half(expert_key, 0, width), own_half(expert_value, 0, width)], axis=0)
    pair = [pair, pair]
    rest = [own_half(expert_query, i * width, width) for i in range(strips - 1)]
    rest = jnp.concatenate([*rest, expert_query[:, (strips - 1) * width :]], axis=0)
    rest = [rest, rest]
    for k in range(1, half + 1):
        entries = [k, half + k] if k < half else [half, half]
        if k == half:
            pair, rest = [pair[0][:part], pair[1][part:]], [rest[0][:cut], rest[1][cut:]]
        pair, rest = around(pair), around(rest)
        crossed = across(pair) if shared else []
        for side, arrays in ((group, [(a, 0) for a in pair]), (1, crossed)):
            for i, ((array, base), entry) in enumerate(zip(arrays, entries)):
                for segment in range(2) if k < half else [i]:
                    low = base + (segment * part if k < half else 0)
                    kv_plan.add(array, low, part, entry, segment, 0, side)
        split = rest if k < half else rest[:1]
        crossed = across(split, cut) if shared else []
        arrays = [(a, 0) for a in (rest if k < half else rest[:1])]
        for side, arrays in ((group, arrays), (1, crossed)):
            for (array, base), entry in zip(arrays, entries):
                for segment in range(strips - 1):
                    query_plan.add(array, base + segment * part, part, entry, segment, 0, side)
        for array, entry in zip(rest if k < half else rest[1:], entries):
            query_plan.add(array, cut if k < half else 0, rows, entry, strips - 1)

    out_plan = Plan(out_rows, out_cols, 1)
    out_plan.add(expert_out, 0, out_rows, 0, 0)
    out_part = out_rows // 2 if shared else out_rows
    message = expert_out
    if shared:
        message = lax.dynamic_slice_in_dim(expert_out, lax.axis_index("groups") * out_part, out_part)
    for k, pair, entries in ring(message, out_part // 2):
        crossed = across(pair) if shared else []
        size = pair[0].shape[0]
        for side, arrays in ((group, [(a, 0) for a in pair]), (1, crossed)):
            for i, ((array, base), entry) in enumerate(zip(arrays, entries)):
                offset = i * (out_part // 2) if k == half else 0
                out_plan.add(array, base, size, entry, 0, offset, side)

    other_states = lax.ppermute(prefix_states, "col", swap)
    other_actions = lax.ppermute(action_states, "col", swap)
    partial = prefix_partial(
        spot, at, prefix_states, other_states, prefix_gain, backbone_key, backbone_value
    )
    block = partial.shape[0] // count
    key_cols = backbone_key.shape[1]
    full = partial.shape[1]
    far = spot(at[0]).owner(half) * block
    sums = [
        lax.dynamic_slice(partial, (far, 0), (block, key_cols)),
        lax.dynamic_slice(partial, (far, key_cols), (block, full - key_cols)),
    ]
    for k in range(1, half + 1):
        got = around(sums)
        if k < half:
            sums = reduce_call(
                reduce_step_kernel,
                spot,
                at,
                partial,
                block,
                [2 * half - k, half - k],
                got,
                [full] * 2,
            )
        else:
            prefix_keys, prefix_values, keys_near, values_near = reduce_call(
                reduce_last_kernel, spot, at, partial, block, [0], got, [key_cols] * 4
            )

    states = (action_states, other_actions)
    key, value = project(spot, at, *states, kv_plan, [width, width])
    (query,) = project(spot, at, *states, query_plan, [query_cols], HEAD**-0.5 * LOG2E)

    groups = width // HEAD
    at_once = max(groups // 2, 1)
    attended = []
    for first in range(0, groups, at_once):
        attended.append(
            attend(
                prefix_length,
                action_length,
                query,
                key,
                value,
                keys_near,
                values_near,
                first,
                at_once,
            )
        )

    tokens = action_states.shape[0]

    def outward(side, dtype):
        return project_out(spot, at, attended, out_plan, out_rows, half, (), tokens, side, dtype)

    given = lax.ppermute(outward(1, bf16), "col", swap)
    action_out = add(outward(0, f32), given)
    return (prefix_keys, prefix_values, action_out)


def shares(replicas, rows):
    return replicas == 2 and rows % 256 == 0


def solution(mesh):
    placed = (
        P(("groups", "col"), "row"),
        P("row"),
        P("row", "col"),
        P("row", "col"),
        P(("groups", "row"), "col"),
        P("row", "col"),
        P("row", "col"),
        P("row", "col"),
        P("col", "row"),
        P(("groups", "row")),
        P(("groups", "row")),
    )
    count, replicas = mesh.shape["row"], mesh.shape["groups"]

    def body(*args):
        return shards(count, replicas, *args)

    return jax.shard_map(
        body,
        mesh=mesh,
        in_specs=placed,
        out_specs=(
            P(("groups", "row"), "col"),
            P(("groups", "row"), "col"),
            P(("groups", "row"), "col"),
        ),
        check_vma=False,
    )
```
